32 devices in a mesh: parts: 2 (over y), tile: 4 (over z), src: 2 (over x), focus: 2 (over core).
Axes of the slice: x: 2, y: 2, z: 4, core: 2. Of those that a mesh axis runs over, the one named last changes fastest.
Arguments:
- mask: float32 [768, 1536], P('parts', 'tile'), parts along dimension 0, may hold values from -1 to 1
- target: float32 [768, 1536], P('parts', 'tile'), parts along dimension 0, may hold values from 0 to 1
- pupil: float32 [2, 16, 4, 64, 64], P(None, 'src', 'focus'), may hold values from -6 to 6
- weights: float32 [16], P('src'), may hold values from 0.25 to 4
- counts: int32 [8], P('parts'), parts along dimension 0, may hold values from 1 to 4, as said below
Outputs:
- gradient: float32 [768, 1536], P(('parts', 'src', 'focus'), 'tile'), parts along dimension 0
The draws below stay inside these ranges and needn't reach their ends.
There are 2 independent parts, one for each index of `parts`. The reference program is written for one: setup_inputs(seed, part) draws one part's arguments, and reference() takes and returns one part's arrays. A program takes and returns all parts, laid end to end along the dimension named above; an argument that names none is the same for every part. Nothing has to cross between parts.
Inputs may be any that keep to these rules, and one draw needn't show every extreme that they name: Corners 0 to counts - 1 of a subtile are in use; of the two subtiles t and t + 2 at least one uses a single corner; some subtile uses all 4.
All inputs are finite; a program needn't handle non-finite values.
Results may differ from the reference program's by a relative error of at most 0.0003.
Values sent between devices are 32-bit elements; how exact they have to be, the bound alone decides.
No kernel may reach another device: no remote copies, remote signals or barrier semaphores. Data moves between devices by JAX's collectives and lax.ppermute only.
A program may use at most 128 MiB of HBM per device.

```python
import math
import jax
import jax.numpy as jnp
from jax import lax

TILE = 384
AMBIT = 64
KF = 64
CMAX = 4
WIN = 512
SOURCES = 16
TILES = 4


def draw_counts(key, part):
    half = TILES // 2
    dense = jax.random.randint(key, (half,), 1, CMAX + 1)
    order = jax.random.permutation(jax.random.fold_in(key, 7), half)
    dense = dense.at[order[0]].set(CMAX)
    which = jax.random.randint(jax.random.fold_in(key, 11), (half,), 0, 2)
    single = jnp.ones((half,), jnp.int32)
    lower = jnp.where(which == 0, dense, single)
    upper = jnp.where(which == 0, single, dense)
    return jnp.concatenate([lower, upper]).astype(jnp.int32)


def block_scale(key, extent, pieces, least, high):
    gain, own = 1.0, jax.random.fold_in(key, 6)
    for position, shards_of in pieces:
        steps = jnp.exp(jax.random.uniform(jax.random.fold_in(own, position), (shards_of,), jnp.float32, least / len(pieces), high / len(pieces)))
        gain = gain * jnp.repeat(steps, extent[position] // shards_of).reshape([-1 if axis == position else 1 for axis in range(len(extent))])
    return gain


def scatter_about(rng, extent, width, most, pieces=(), kind=jnp.bfloat16):
    result = width * jax.random.normal(rng, extent, jnp.float32)
    if pieces:
        result = result * block_scale(rng, extent, pieces, -0.22, 0.18)
    return jnp.clip(result, -most, most).astype(kind)


def setup_inputs(seed: int = 0, part: int = 0) -> dict:
    streams_of = jax.random.split(jax.random.key(seed), 6)
    own_keys = jax.random.split(jax.random.fold_in(streams_of[5], part), 6)
    mask = jnp.clip(jax.random.uniform(own_keys[0], (TILE, TILES * TILE), jnp.float32, -1.0, 1.0) * block_scale(own_keys[0], (TILE, TILES * TILE), ((1, 4),), -0.4, 0.0), -1.0, 1.0)
    target = jnp.clip(1.0 * jax.random.uniform(own_keys[1], (TILE, TILES * TILE), jnp.float32) ** block_scale(own_keys[1], (TILE, TILES * TILE), ((1, 4),), -0.2, 0.2), 0.0, 1.0)
    pupil = scatter_about(streams_of[2], (2, SOURCES, CMAX, KF, KF), 1.0, 6.0, ((1, 2), (2, 2)), jnp.float32)
    weights = jnp.clip(jnp.exp(math.log(4.0) - 2.7725887 * jax.random.uniform(streams_of[3], (SOURCES,), jnp.float32) ** block_scale(streams_of[3], (SOURCES,), ((0, 2),), -0.2, 0.2)), 0.25, 4.0)
    counts = draw_counts(jax.random.fold_in(jax.random.fold_in(streams_of[5], part), 71), part)
    return {"mask": mask, "target": target, "pupil": pupil, "weights": weights, "counts": counts}


resist_slope = 4.0
resist_level = 0.5

def product(left, right):
    return jnp.dot(left, right, precision=lax.Precision.HIGHEST, preferred_element_type=jnp.float32)

def contract(form, left, right):
    return jnp.einsum(form, left, right, precision=lax.Precision.HIGHEST, preferred_element_type=jnp.float32)

def phase_table(freqs, length, offset, count):
    kvalues = jnp.arange(freqs, dtype=jnp.int32) - freqs // 2
    nvalues = jnp.arange(count, dtype=jnp.int32) + offset
    phase = jnp.mod(kvalues[:, None] * nvalues[None, :], length).astype(jnp.float32) * (2.0 * math.pi / length)
    return (jnp.cos(phase), jnp.sin(phase))

def reference(mask, target, pupil, weights, counts):
    norm_win = 1.0 / math.sqrt(WIN)
    norm_back = math.sqrt(2.0 / KF)
    cos_col, sin_col = phase_table(KF, WIN, 0, WIN)
    col_re = cos_col * norm_win
    col_im = -sin_col * norm_win
    cos_row, sin_row = phase_table(KF, WIN, AMBIT, TILE)
    row_re = cos_row * norm_win
    row_im = -sin_row * norm_win
    back_re = cos_row.T * norm_back
    back_im = sin_row.T * norm_back
    padded = jnp.pad(mask, ((0, 0), (AMBIT, AMBIT)))
    pup_re = pupil[0]
    pup_im = pupil[1]
    src_scale = weights / SOURCES
    corner_ids = jnp.arange(CMAX, dtype=jnp.int32)

    def one_tile(tile_index):
        window = lax.dynamic_slice_in_dim(padded, tile_index * TILE, WIN, 1)
        x_re = product(window, col_re.T)
        x_im = product(window, col_im.T)
        spec_re = product(row_re, x_re) - product(row_im, x_im)
        spec_im = product(row_re, x_im) + product(row_im, x_re)
        g_re = pup_re * spec_re - pup_im * spec_im
        g_im = pup_re * spec_im + pup_im * spec_re
        h_re = contract('sckl,nl->sckn', g_re, back_re) - contract('sckl,nl->sckn', g_im, back_im)
        h_im = contract('sckl,nl->sckn', g_re, back_im) + contract('sckl,nl->sckn', g_im, back_re)
        e_re = contract('mk,sckn->scmn', back_re, h_re) - contract('mk,sckn->scmn', back_im, h_im)
        e_im = contract('mk,sckn->scmn', back_re, h_im) + contract('mk,sckn->scmn', back_im, h_re)
        intensity = contract('s,scmn->cmn', src_scale, e_re * e_re + e_im * e_im)
        resist = jax.nn.sigmoid(resist_slope * (intensity - resist_level))
        tgt = lax.dynamic_slice_in_dim(target, tile_index * TILE, TILE, 1)
        active = (corner_ids < counts[tile_index]).astype(jnp.float32)
        slope = 2.0 * (resist - tgt[None]) * resist_slope * resist * (1.0 - resist) * active[:, None, None]
        factor = 2.0 * src_scale[:, None, None, None] * slope[None]
        ge_re = factor * e_re
        ge_im = factor * e_im
        gh_re = contract('mk,scmn->sckn', back_re, ge_re) + contract('mk,scmn->sckn', back_im, ge_im)
        gh_im = contract('mk,scmn->sckn', back_re, ge_im) - contract('mk,scmn->sckn', back_im, ge_re)
        gg_re = contract('sckn,nl->sckl', gh_re, back_re) + contract('sckn,nl->sckl', gh_im, back_im)
        gg_im = contract('sckn,nl->sckl', gh_im, back_re) - contract('sckn,nl->sckl', gh_re, back_im)
        gs_re = lax.optimization_barrier(jnp.sum(pup_re * gg_re + pup_im * gg_im, axis=(0, 1)))
        gs_im = lax.optimization_barrier(jnp.sum(pup_re * gg_im - pup_im * gg_re, axis=(0, 1)))
        gx_re = product(row_re.T, gs_re) + product(row_im.T, gs_im)
        gx_im = product(row_re.T, gs_im) - product(row_im.T, gs_re)
        return product(gx_re, col_re) + product(gx_im, col_im)

    def accumulate(tile_index, total):
        piece = one_tile(tile_index)
        start = (tile_index * TILE).astype(jnp.int32)
        zero = jnp.zeros((), jnp.int32)
        current = lax.dynamic_slice(total, (zero, start), (TILE, WIN))
        return lax.dynamic_update_slice(total, current + piece, (zero, start))
    total = jnp.zeros((TILE, TILES * TILE + 2 * AMBIT), jnp.float32)
    total = lax.fori_loop(0, TILES, accumulate, total)
    return total[:, AMBIT:AMBIT + TILES * TILE]
```

```python
import math

import jax
import jax.numpy as jnp
import numpy as np
from jax import lax
from jax.experimental import pallas as pl
from jax.experimental.pallas import tpu as pltpu
from jax.sharding import PartitionSpec as P

AMBIT = 64

RESIST_SLOPE = 4.0
RESIST_LEVEL = 0.5

VMEM = pl.BlockSpec(memory_space=pltpu.VMEM)
SMEM = pl.BlockSpec(memory_space=pltpu.SMEM)


def halves(value):
    value = np.asarray(value, np.float32)
    high = value.astype(jnp.bfloat16)
    low = (value - high.astype(np.float32)).astype(jnp.bfloat16)
    return np.stack([high, low])


def split(value):
    high = value.astype(jnp.bfloat16)
    low = (value - high.astype(jnp.float32)).astype(jnp.bfloat16)
    return high, low


def mm(left, right):
    return lax.dot_general(
        left, right, (((1,), (0,)), ((), ())), preferred_element_type=jnp.float32
    )


def mm3(left, right):
    lh, ll = left
    rh, rl = right
    return mm(jnp.concatenate([lh, ll, lh], axis=1), jnp.concatenate([rh, rh, rl], axis=0))


def phase(freqs, length, positions):
    k = np.arange(freqs) - freqs // 2
    angle = np.mod(k[:, None] * np.asarray(positions)[None, :], length) * (2.0 * math.pi / length)
    return np.cos(angle), np.sin(angle)


def make_tables(tile, freqs, width):
    win = tile + 2 * width
    grid = 2 * freqs
    norm_win = 1.0 / math.sqrt(win)
    norm_back = math.sqrt(2.0 / freqs)
    cos_col, sin_col = phase(freqs, win, np.arange(win))
    col_re, col_im = cos_col * norm_win, -sin_col * norm_win
    cos_row, sin_row = phase(freqs, win, np.arange(tile) + width)
    row_re, row_im = cos_row * norm_win, -sin_row * norm_win
    cos_grid, sin_grid = phase(freqs, grid, np.arange(grid))
    a_re, a_im = cos_grid.T * norm_back, sin_grid.T * norm_back

    row = np.concatenate([row_re, row_im], axis=0)
    colt = np.concatenate([col_re.T, col_im.T], axis=1)
    side = max(128, width)
    edge = np.zeros((2, side, 2 * freqs))
    edge[0, side - width :] = colt[:width]
    edge[1, :width] = colt[win - width :]

    right1 = np.block([[a_re.T, a_im.T], [-a_im.T, a_re.T]])
    left2 = np.concatenate([a_re, a_im], axis=0)
    back2 = np.concatenate([a_re.T, a_im.T], axis=0)

    q = np.arange(-(freqs - 1), freqs)
    at = (np.arange(tile) + width)[:, None] / win - np.arange(grid)[None, :] / grid
    up = np.cos(2.0 * math.pi * at[:, :, None] * q).sum(-1) / grid

    l2h, l2l = halves(left2)
    b2h, b2l = halves(back2)
    return dict(
        row=halves(row),
        colt=halves(colt[width : width + tile]),
        edge=np.stack([halves(edge[0]), halves(edge[1])]),
        right1=halves(right1),
        left2=np.concatenate([l2h, l2h, l2l], axis=1),
        back2=np.block([[b2h, b2h], [b2l, b2l]]),
        up=halves(up),
        upt=halves(up.T),
        rowt=halves(row.T),
        colown=halves(np.concatenate([col_re, col_im], 0)[:, width : width + tile]),
        coledge=np.stack([halves(edge[0].T), halves(edge[1].T)]),
    )


def swapped_halves(x):
    return pltpu.roll(x, x.shape[-1] // 2, x.ndim - 1)


def left_lanes(shape):
    return lax.broadcasted_iota(jnp.int32, shape, len(shape) - 1) < shape[-1] // 2


def as_spectrum(z):
    half = z.shape[0] // 2
    turned = swapped_halves(z[half:])
    return z[:half] + jnp.where(left_lanes(turned.shape), -turned, turned)


def pack(pupil_ref, source, corner, scale):
    re = pupil_ref[0, source, corner] * scale
    im = pupil_ref[1, source, corner] * scale
    return jnp.concatenate([re, im], axis=1)


def source_scale(weights_ref, source, sources):
    w = jnp.full((1, 1), weights_ref[source], jnp.float32)
    return jnp.sqrt(w / sources)


def send_kernel(sources, where_ref, weights_ref, pupil_ref, out_ref):
    for d in range(out_ref.shape[0]):
        for s in range(out_ref.shape[1]):
            scale = source_scale(weights_ref, s, sources)
            out_ref[d, s] = pack(pupil_ref, s, where_ref[1 + d], scale)


def edge_kernel(where_ref, mask_ref, row_ref, edge_ref, out_ref):
    side = edge_ref.shape[2]
    focus = where_ref[0]
    start = pl.multiple_of((1 - focus) * (mask_ref.shape[1] - side), 128)
    slab = split(mask_ref[:, pl.ds(start, side)])
    y = mm3((row_ref[0], row_ref[1]), slab)
    out_ref[...] = as_spectrum(mm3(split(y), (edge_ref[focus, 0], edge_ref[focus, 1])))


def own_kernel(
    sources, where_ref, weights_ref, pupil_ref, mask_ref, row_ref, colt_ref, spec_ref, pack_ref
):
    y = mm3((row_ref[0], row_ref[1]), split(mask_ref[...]))
    spec_ref[...] = as_spectrum(mm3(split(y), (colt_ref[0], colt_ref[1])))
    for s in range(pack_ref.shape[0]):
        scale = source_scale(weights_ref, s, sources)
        pack_ref[s] = pack(pupil_ref, s, where_ref[0], scale)


def forward(spec, pupil_of, count, right1_ref, left2_ref, field_ref):
    freqs, grid = spec.shape[0], right1_ref.shape[2] // 2
    turned = swapped_halves(spec)
    low = left_lanes(spec.shape)
    spec_a = jnp.where(low, spec, turned)
    spec_b = jnp.where(low, -turned, spec)
    right1 = (right1_ref[0], right1_ref[1])
    left2 = left2_ref[...]
    total = jnp.zeros((grid, grid), jnp.float32)
    for s in range(count):
        p = pupil_of(s)
        g = p * spec_a + swapped_halves(p) * spec_b
        hh, hl = split(mm3(split(g), right1))
        f = mm(left2, jnp.concatenate([hh, hl, hh], axis=0))
        e_re = f[:grid, :grid] - f[grid:, grid:]
        e_im = f[:grid, grid:] + f[grid:, :grid]
        field_ref[s, :, :grid] = e_re
        field_ref[s, :, grid:] = e_im
        total = total + (e_re * e_re + e_im * e_im)
    return total


def adjoint(intensity, target, active, pupil_of, count, right1t, back2_ref, up, upt, field_ref):
    grid = intensity.shape[0]
    freqs = grid // 2
    image = mm3(up, split(mm3(split(intensity), upt)))
    resist = jax.nn.sigmoid(RESIST_SLOPE * (image - RESIST_LEVEL))
    slope = 2.0 * (resist - target) * RESIST_SLOPE * resist * (1.0 - resist)
    down = mm3(split(mm3(upt, split(slope))), up) * (2.0 * active)
    down2 = jnp.concatenate([down, down], axis=1)
    back2 = back2_ref[...]
    th, tl = right1t
    both = jnp.concatenate([th, tl], axis=1)
    t1 = jnp.zeros((freqs, 2 * freqs), jnp.float32)
    t2 = jnp.zeros((freqs, 2 * freqs), jnp.float32)
    for s in range(count):
        eh, el = split(down2 * field_ref[s])
        f = mm(back2, jnp.concatenate([eh, el], axis=0))
        f = f[: 2 * freqs] + f[2 * freqs :]
        h = jnp.concatenate(
            [f[:freqs, :grid] + f[freqs:, grid:], f[:freqs, grid:] - f[freqs:, :grid]], axis=1
        )
        hh, hl = split(h)
        q = mm(hh, both)
        q = q[:, : 2 * freqs] + q[:, 2 * freqs :] + mm(hl, th)
        p = pupil_of(s)
        t1 = t1 + p * q
        t2 = t2 + swapped_halves(p) * q
    low = left_lanes(t1.shape)
    return jnp.where(low, t1 + swapped_halves(t1), t2 - swapped_halves(t2))


def pick(packs):
    local = packs[0].shape[0]
    return lambda s: packs[s // local][s % local]


def main_kernel(n_spec, n_pack, active_ref, *refs):
    specs, refs = refs[:n_spec], refs[n_spec:]
    packs, refs = refs[:n_pack], refs[n_pack:]
    target_ref, right1_ref, right1t_ref, left2_ref, back2_ref, up_ref, upt_ref = refs[:7]
    out_ref, field_ref = refs[7:]
    spec = sum(ref[...] for ref in specs[1:]) + specs[0][...]
    pupil_of = pick(packs)
    count = n_pack * packs[0].shape[0]
    intensity = forward(spec, pupil_of, count, right1_ref, left2_ref, field_ref)
    out_ref[...] = adjoint(
        intensity,
        target_ref[...],
        active_ref[0],
        pupil_of,
        count,
        (right1t_ref[0], right1t_ref[1]),
        back2_ref,
        (up_ref[0], up_ref[1]),
        (upt_ref[0], upt_ref[1]),
        field_ref,
    )


def forward_kernel(n_spec, n_pack, *refs):
    specs, refs = refs[:n_spec], refs[n_spec:]
    packs, refs = refs[:n_pack], refs[n_pack:]
    right1_ref, left2_ref, intensity_ref, field_ref = refs
    spec = sum(ref[...] for ref in specs[1:]) + specs[0][...]
    count = n_pack * packs[0].shape[0]
    intensity_ref[...] = forward(spec, pick(packs), count, right1_ref, left2_ref, field_ref)


def adjoint_kernel(n_part, n_pack, active_ref, *refs):
    parts, refs = refs[:n_part], refs[n_part:]
    packs, refs = refs[:n_pack], refs[n_pack:]
    target_ref, right1t_ref, back2_ref, up_ref, upt_ref, field_ref, out_ref = refs
    out_ref[...] = adjoint(
        sum(ref[...] for ref in parts[1:]) + parts[0][...],
        target_ref[...],
        active_ref[0],
        pick(packs),
        n_pack * packs[0].shape[0],
        (right1t_ref[0], right1t_ref[1]),
        back2_ref,
        (up_ref[0], up_ref[1]),
        (upt_ref[0], upt_ref[1]),
        field_ref,
    )


def final_kernel(n_own, n_near, where_ref, *refs):
    own, refs = refs[:n_own], refs[n_own:]
    near, refs = refs[:n_near], refs[n_near:]
    across_ref, rowt_ref, colown_ref, coledge_ref, out_ref = refs
    rows, tile = out_ref.shape
    side = coledge_ref.shape[3]
    focus = where_ref[0]
    start = pl.multiple_of(where_ref[1] * rows, rows)
    rowt = (rowt_ref[0, pl.ds(start, rows)], rowt_ref[1, pl.ds(start, rows)])

    def lines(gs):
        turned = swapped_halves(gs)
        stack = jnp.concatenate([gs, jnp.where(left_lanes(gs.shape), turned, -turned)], axis=0)
        return split(mm3(rowt, split(stack)))

    received = sum(ref[...] for ref in near[1:]) + near[0][...]
    across = across_ref[...]
    first = focus == 0
    from_right = jnp.where(first, received, across)
    from_left = jnp.where(first, across, received)
    main = mm3(lines(sum(ref[...] for ref in own[1:]) + own[0][...]), (colown_ref[0], colown_ref[1]))
    high = mm3(lines(from_right), (coledge_ref[0, 0], coledge_ref[0, 1]))
    low = mm3(lines(from_left), (coledge_ref[1, 0], coledge_ref[1, 1]))
    out_ref[...] = main
    out_ref[:, :side] = out_ref[:, :side] + low
    out_ref[:, tile - side :] = out_ref[:, tile - side :] + high


def call(kernel, shapes, specs, scratch=()):
    many = isinstance(shapes, (list, tuple))
    return pl.pallas_call(
        kernel,
        out_shape=[jax.ShapeDtypeStruct(s, jnp.float32) for s in shapes]
        if many
        else jax.ShapeDtypeStruct(shapes.shape, jnp.float32),
        in_specs=specs,
        out_specs=[VMEM] * len(shapes) if many else VMEM,
        scratch_shapes=list(scratch),
    )


class Shape:
    def __init__(self, *shape):
        self.shape = shape


def per_device(mask, target, pupil, weights, counts):
    tile = mask.shape[0]
    freqs = pupil.shape[-1]
    grid = 2 * freqs
    local_src = weights.shape[0]
    corner_dev = pupil.shape[2]
    n_tile, n_src, n_focus = (lax.axis_size(a) for a in ("tile", "src", "focus"))
    sources = local_src * n_src
    group = corner_dev if n_src % corner_dev == 0 else 1
    n_corner = corner_dev // group
    assert n_focus == 2
    t_index, s_index, f_index = (lax.axis_index(a) for a in ("tile", "src", "focus"))
    rank = s_index % group
    i32 = jnp.int32
    tables = {name: jnp.asarray(value) for name, value in make_tables(tile, freqs, AMBIT).items()}
    tables["right1t"] = jnp.asarray(
        np.swapaxes(np.asarray(make_tables(tile, freqs, AMBIT)["right1"]), 1, 2)
    )

    def hop_src(value, by):
        return lax.ppermute(value, "src", [(i, (i + by) % n_src) for i in range(n_src)])

    def hop_group(value, by):
        pairs = [(i, i // group * group + (i + by) % group) for i in range(n_src)]
        return lax.ppermute(value, "src", pairs)

    def hop_focus(value):
        return lax.ppermute(value, "focus", [(0, 1), (1, 0)])

    def hop_tile(value, by):
        def place(t, s, f):
            return (t * n_src + s) * n_focus + f

        pairs = []
        for t in range(n_tile - 1):
            for s in range(n_src):
                u = (s + by) % n_src
                pairs.append((place(t, s, 0), place(t + 1, u, 1)))
                pairs.append((place(t + 1, s, 1), place(t, u, 0)))
        return lax.ppermute(value, ("tile", "src", "focus"), pairs)

    got = []
    if group > 1:
        where = jnp.stack([f_index] + [(rank + d) % group for d in range(1, group)]).astype(i32)
        sends = call(
            lambda *refs: send_kernel(sources, *refs),
            Shape(group - 1, local_src, freqs, 2 * freqs),
            [SMEM, SMEM, VMEM],
        )(where, weights, pupil)
        got = [hop_group(sends[d - 1], d) for d in range(1, group)]
    edge = call(edge_kernel, Shape(freqs, 2 * freqs), [SMEM, VMEM, VMEM, VMEM])(
        jnp.stack([f_index]).astype(i32), mask, tables["row"], tables["edge"]
    )
    near = hop_tile(edge, 0)
    spec, own_pack = call(
        lambda *refs: own_kernel(sources, *refs),
        [(freqs, 2 * freqs), (local_src, freqs, 2 * freqs)],
        [SMEM, SMEM, VMEM, VMEM, VMEM, VMEM],
    )(jnp.stack([rank]).astype(i32), weights, pupil, mask, tables["row"], tables["colt"])
    specs = [spec, near, hop_focus(near)]

    gradient = []
    for c in range(n_corner):
        if group > 1:
            packs = [own_pack] + got
            corner = f_index * corner_dev + rank
        else:
            packs = [
                call(
                    lambda *refs: send_kernel(sources, *refs),
                    Shape(1, local_src, freqs, 2 * freqs),
                    [SMEM, SMEM, VMEM],
                )(jnp.array([0, c], i32), weights, pupil)[0]
            ]
            corner = f_index * corner_dev + c
        active = (corner < counts[t_index]).astype(jnp.float32)[None]
        n_pack = len(packs)
        field = (n_pack * local_src, grid, 2 * grid)
        if n_src == group:
            gs = call(
                lambda *refs: main_kernel(len(specs), n_pack, *refs),
                Shape(freqs, 2 * freqs),
                [SMEM] + [VMEM] * (len(specs) + n_pack + 7),
                [pltpu.VMEM(field, jnp.float32)],
            )(
                active,
                *specs,
                *packs,
                target,
                *(tables[k] for k in ("right1", "right1t", "left2", "back2", "up", "upt")),
            )
        else:
            part, fields = call(
                lambda *refs: forward_kernel(len(specs), n_pack, *refs),
                [(grid, grid), field],
                [VMEM] * (len(specs) + n_pack + 2),
            )(*specs, *packs, tables["right1"], tables["left2"])
            parts = [part] + [hop_src(part, r) for r in range(group, n_src, group)]
            gs = call(
                lambda *refs: adjoint_kernel(len(parts), n_pack, *refs),
                Shape(freqs, 2 * freqs),
                [SMEM] + [VMEM] * (len(parts) + n_pack + 6),
            )(
                active,
                *parts,
                *packs,
                target,
                *(tables[k] for k in ("right1t", "back2", "up", "upt")),
                fields,
            )
        gradient.append(gs)
    gs = sum(gradient[1:]) + gradient[0] if len(gradient) > 1 else gradient[0]
    gs = gs + hop_focus(gs)
    own = [gs] + [hop_src(gs, d) for d in range(1, n_src)]
    near = [hop_tile(gs, d) for d in range(n_src)]
    received = sum(near[1:]) + near[0] if len(near) > 1 else near[0]
    across = hop_focus(received)
    rows = tile // (n_src * n_focus)
    where = jnp.stack([f_index, s_index * n_focus + f_index]).astype(i32)
    return call(
        lambda *refs: final_kernel(len(own), 1, *refs),
        Shape(rows, tile),
        [SMEM] + [VMEM] * (len(own) + 5),
    )(
        where,
        *own,
        received,
        across,
        *(tables[k] for k in ("rowt", "colown", "coledge")),
    )


def solution(mesh):
    return jax.shard_map(
        per_device,
        mesh=mesh,
        in_specs=(
            P("parts", "tile"),
            P("parts", "tile"),
            P(None, "src", "focus", None, None),
            P("src"),
            P("parts"),
        ),
        out_specs=P(("parts", "src", "focus"), "tile"),
        check_vma=False,
    )
```

```python
import math

import jax
import jax.numpy as jnp
import numpy as np
from jax import lax
from jax.experimental import pallas as pl
from jax.experimental.pallas import tpu as pltpu
from jax.sharding import PartitionSpec as P

AMBIT = 64

RESIST_SLOPE = 4.0
RESIST_LEVEL = 0.5

VMEM = pl.BlockSpec(memory_space=pltpu.VMEM)
SMEM = pl.BlockSpec(memory_space=pltpu.SMEM)


def halves(value):
    value = np.asarray(value, np.float32)
    high = value.astype(jnp.bfloat16)
    low = (value - high.astype(np.float32)).astype(jnp.bfloat16)
    return np.stack([high, low])


def split(value):
    high = value.astype(jnp.bfloat16)
    low = (value - high.astype(jnp.float32)).astype(jnp.bfloat16)
    return high, low


def mm(left, right):
    return lax.dot_general(
        left, right, (((1,), (0,)), ((), ())), preferred_element_type=jnp.float32
    )


def mm3(left, right):
    lh, ll = left
    rh, rl = right
    return mm(jnp.concatenate([lh, ll, lh], axis=1), jnp.concatenate([rh, rh, rl], axis=0))


def phase(freqs, length, positions):
    k = np.arange(freqs) - freqs // 2
    angle = np.mod(k[:, None] * np.asarray(positions)[None, :], length) * (2.0 * math.pi / length)
    return np.cos(angle), np.sin(angle)


def make_tables(tile, freqs, width):
    win = tile + 2 * width
    grid = 2 * freqs
    norm_win = 1.0 / math.sqrt(win)
    norm_back = math.sqrt(2.0 / freqs)
    cos_col, sin_col = phase(freqs, win, np.arange(win))
    col_re, col_im = cos_col * norm_win, -sin_col * norm_win
    cos_row, sin_row = phase(freqs, win, np.arange(tile) + width)
    row_re, row_im = cos_row * norm_win, -sin_row * norm_win
    cos_grid, sin_grid = phase(freqs, grid, np.arange(grid))
    a_re, a_im = cos_grid.T * norm_back, sin_grid.T * norm_back

    row = np.concatenate([row_re, row_im], axis=0)
    colt = np.concatenate([col_re.T, col_im.T], axis=1)
    side = max(128, width)
    edge = np.zeros((2, side, 2 * freqs))
    edge[0, side - width :] = colt[:width]
    edge[1, :width] = colt[win - width :]

    right1 = np.block([[a_re.T, a_im.T], [-a_im.T, a_re.T]])
    left2 = np.concatenate([a_re, a_im], axis=0)
    back2 = np.concatenate([a_re.T, a_im.T], axis=0)

    q = np.arange(-(freqs - 1), freqs)
    at = (np.arange(tile) + width)[:, None] / win - np.arange(grid)[None, :] / grid
    up = np.cos(2.0 * math.pi * at[:, :, None] * q).sum(-1) / grid

    l2h, l2l = halves(left2)
    b2h, b2l = halves(back2)
    return dict(
        row=halves(row),
        colt=halves(colt[width : width + tile]),
        edge=np.stack([halves(edge[0]), halves(edge[1])]),
        right1=halves(right1),
        left2=np.concatenate([l2h, l2h, l2l], axis=1),
        back2=np.block([[b2h, b2h], [b2l, b2l]]),
        up=halves(up),
        upt=halves(up.T),
        rowt=halves(row.T),
        colown=halves(np.concatenate([col_re, col_im], 0)[:, width : width + tile]),
        coledge=np.stack([halves(edge[0].T), halves(edge[1].T)]),
    )


def swapped_halves(x):
    return pltpu.roll(x, x.shape[-1] // 2, x.ndim - 1)


def left_lanes(shape):
    return lax.broadcasted_iota(jnp.int32, shape, len(shape) - 1) < shape[-1] // 2


def as_spectrum(z):
    half = z.shape[0] // 2
    turned = swapped_halves(z[half:])
    return z[:half] + jnp.where(left_lanes(turned.shape), -turned, turned)


def pack(pupil_ref, source, corner, scale):
    re = pupil_ref[0, source, corner] * scale
    im = pupil_ref[1, source, corner] * scale
    return jnp.concatenate([re, im], axis=1)


def source_scale(weights_ref, source, sources):
    w = jnp.full((1, 1), weights_ref[source], jnp.float32)
    return jnp.sqrt(w / sources)


def send_kernel(sources, corner_of, weights_ref, pupil_ref, out_ref):
    for d in range(out_ref.shape[0]):
        for s in range(out_ref.shape[1]):
            scale = source_scale(weights_ref, s, sources)
            out_ref[d, s] = pack(pupil_ref, s, corner_of(d), scale)


def edge_kernel(mask_ref, row_ref, edge_ref, out_ref):
    side = edge_ref.shape[2]
    focus = lax.axis_index("focus")
    start = pl.multiple_of((1 - focus) * (mask_ref.shape[1] - side), 128)
    slab = split(mask_ref[:, pl.ds(start, side)])
    y = mm3((row_ref[0], row_ref[1]), slab)
    out_ref[...] = as_spectrum(mm3(split(y), (edge_ref[focus, 0], edge_ref[focus, 1])))


def own_kernel(
    sources, corner_of, weights_ref, pupil_ref, mask_ref, row_ref, colt_ref, spec_ref, pack_ref
):
    y = mm3((row_ref[0], row_ref[1]), split(mask_ref[...]))
    spec_ref[...] = as_spectrum(mm3(split(y), (colt_ref[0], colt_ref[1])))
    for s in range(pack_ref.shape[0]):
        scale = source_scale(weights_ref, s, sources)
        pack_ref[s] = pack(pupil_ref, s, corner_of(0), scale)


def forward(spec, pupil_of, count, right1_ref, left2_ref, field_ref):
    freqs, grid = spec.shape[0], right1_ref.shape[2] // 2
    turned = swapped_halves(spec)
    low = left_lanes(spec.shape)
    spec_a = jnp.where(low, spec, turned)
    spec_b = jnp.where(low, -turned, spec)
    right1 = (right1_ref[0], right1_ref[1])
    left2 = left2_ref[...]
    total = jnp.zeros((grid, grid), jnp.float32)
    for s in range(count):
        p = pupil_of(s)
        g = p * spec_a + swapped_halves(p) * spec_b
        hh, hl = split(mm3(split(g), right1))
        f = mm(left2, jnp.concatenate([hh, hl, hh], axis=0))
        e_re = f[:grid, :grid] - f[grid:, grid:]
        e_im = f[:grid, grid:] + f[grid:, :grid]
        field_ref[s, :, :grid] = e_re
        field_ref[s, :, grid:] = e_im
        total = total + (e_re * e_re + e_im * e_im)
    return total


def adjoint(intensity, target, active, pupil_of, count, right1t, back2_ref, up, upt, field_ref):
    grid = intensity.shape[0]
    freqs = grid // 2
    image = mm3(up, split(mm3(split(intensity), upt)))
    resist = jax.nn.sigmoid(RESIST_SLOPE * (image - RESIST_LEVEL))
    slope = 2.0 * (resist - target) * RESIST_SLOPE * resist * (1.0 - resist)
    down = mm3(split(mm3(upt, split(slope))), up) * (2.0 * active)
    down2 = jnp.concatenate([down, down], axis=1)
    back2 = back2_ref[...]
    th, tl = right1t
    both = jnp.concatenate([th, tl], axis=1)
    t1 = jnp.zeros((freqs, 2 * freqs), jnp.float32)
    t2 = jnp.zeros((freqs, 2 * freqs), jnp.float32)
    for s in range(count):
        eh, el = split(down2 * field_ref[s])
        f = mm(back2, jnp.concatenate([eh, el], axis=0))
        f = f[: 2 * freqs] + f[2 * freqs :]
        h = jnp.concatenate(
            [f[:freqs, :grid] + f[freqs:, grid:], f[:freqs, grid:] - f[freqs:, :grid]], axis=1
        )
        hh, hl = split(h)
        q = mm(hh, both)
        q = q[:, : 2 * freqs] + q[:, 2 * freqs :] + mm(hl, th)
        p = pupil_of(s)
        t1 = t1 + p * q
        t2 = t2 + swapped_halves(p) * q
    low = left_lanes(t1.shape)
    return jnp.where(low, t1 + swapped_halves(t1), t2 - swapped_halves(t2))


def active_here(corner_of, counts_ref):
    used = counts_ref[lax.axis_index("tile")]
    return (corner_of() < used).astype(jnp.float32)


def pick(packs):
    local = packs[0].shape[0]
    return lambda s: packs[s // local][s % local]


def main_kernel(n_spec, n_pack, corner_of, counts_ref, *refs):
    specs, refs = refs[:n_spec], refs[n_spec:]
    packs, refs = refs[:n_pack], refs[n_pack:]
    target_ref, right1_ref, right1t_ref, left2_ref, back2_ref, up_ref, upt_ref = refs[:7]
    out_ref, field_ref = refs[7:]
    spec = sum(ref[...] for ref in specs[1:]) + specs[0][...]
    pupil_of = pick(packs)
    count = n_pack * packs[0].shape[0]
    intensity = forward(spec, pupil_of, count, right1_ref, left2_ref, field_ref)
    out_ref[...] = adjoint(
        intensity,
        target_ref[...],
        active_here(corner_of, counts_ref),
        pupil_of,
        count,
        (right1t_ref[0], right1t_ref[1]),
        back2_ref,
        (up_ref[0], up_ref[1]),
        (upt_ref[0], upt_ref[1]),
        field_ref,
    )


def forward_kernel(n_spec, n_pack, *refs):
    specs, refs = refs[:n_spec], refs[n_spec:]
    packs, refs = refs[:n_pack], refs[n_pack:]
    right1_ref, left2_ref, intensity_ref, field_ref = refs
    spec = sum(ref[...] for ref in specs[1:]) + specs[0][...]
    count = n_pack * packs[0].shape[0]
    intensity_ref[...] = forward(spec, pick(packs), count, right1_ref, left2_ref, field_ref)


def adjoint_kernel(n_part, n_pack, corner_of, counts_ref, *refs):
    parts, refs = refs[:n_part], refs[n_part:]
    packs, refs = refs[:n_pack], refs[n_pack:]
    target_ref, right1t_ref, back2_ref, up_ref, upt_ref, field_ref, out_ref = refs
    out_ref[...] = adjoint(
        sum(ref[...] for ref in parts[1:]) + parts[0][...],
        target_ref[...],
        active_here(corner_of, counts_ref),
        pick(packs),
        n_pack * packs[0].shape[0],
        (right1t_ref[0], right1t_ref[1]),
        back2_ref,
        (up_ref[0], up_ref[1]),
        (upt_ref[0], upt_ref[1]),
        field_ref,
    )


def final_kernel(n_own, n_near, *refs):
    own, refs = refs[:n_own], refs[n_own:]
    near, refs = refs[:n_near], refs[n_near:]
    across_ref, rowt_ref, colown_ref, coledge_ref, out_ref = refs
    rows, tile = out_ref.shape
    side = coledge_ref.shape[3]
    focus = lax.axis_index("focus")
    strip = lax.axis_index("src") * lax.axis_size("focus") + focus
    start = pl.multiple_of(strip * rows, rows)
    rowt = (rowt_ref[0, pl.ds(start, rows)], rowt_ref[1, pl.ds(start, rows)])

    def lines(gs):
        turned = swapped_halves(gs)
        stack = jnp.concatenate([gs, jnp.where(left_lanes(gs.shape), turned, -turned)], axis=0)
        return split(mm3(rowt, split(stack)))

    received = sum(ref[...] for ref in near[1:]) + near[0][...]
    across = across_ref[...]
    first = focus == 0
    from_right = jnp.where(first, received, across)
    from_left = jnp.where(first, across, received)
    main = mm3(lines(sum(ref[...] for ref in own[1:]) + own[0][...]), (colown_ref[0], colown_ref[1]))
    high = mm3(lines(from_right), (coledge_ref[0, 0], coledge_ref[0, 1]))
    low = mm3(lines(from_left), (coledge_ref[1, 0], coledge_ref[1, 1]))
    out_ref[...] = main
    out_ref[:, :side] = out_ref[:, :side] + low
    out_ref[:, tile - side :] = out_ref[:, tile - side :] + high


def call(kernel, shapes, specs, scratch=(), flops=0, limit=8):
    many = isinstance(shapes, (list, tuple))
    return pl.pallas_call(
        kernel,
        cost_estimate=pl.CostEstimate(flops=flops, bytes_accessed=1 << 20, transcendentals=0),
        compiler_params=pltpu.CompilerParams(vmem_limit_bytes=limit << 20),
        out_shape=[jax.ShapeDtypeStruct(s, jnp.float32) for s in shapes]
        if many
        else jax.ShapeDtypeStruct(shapes.shape, jnp.float32),
        in_specs=specs,
        out_specs=[VMEM] * len(shapes) if many else VMEM,
        scratch_shapes=list(scratch),
    )


class Shape:
    def __init__(self, *shape):
        self.shape = shape


def per_device(mask, target, pupil, weights, counts):
    tile = mask.shape[0]
    freqs = pupil.shape[-1]
    grid = 2 * freqs
    local_src = weights.shape[0]
    corner_dev = pupil.shape[2]
    n_tile, n_src, n_focus = (lax.axis_size(a) for a in ("tile", "src", "focus"))
    sources = local_src * n_src
    group = corner_dev if n_src % corner_dev == 0 else 1
    n_corner = corner_dev // group
    assert n_focus == 2

    def group_corner(d):
        return lax.rem(lax.axis_index("src") + d, group)

    def fixed_corner(c):
        return lambda d: c

    tables = {name: jnp.asarray(value) for name, value in make_tables(tile, freqs, AMBIT).items()}
    tables["right1t"] = jnp.asarray(
        np.swapaxes(np.asarray(make_tables(tile, freqs, AMBIT)["right1"]), 1, 2)
    )

    def hop_src(value, by):
        return lax.ppermute(value, "src", [(i, (i + by) % n_src) for i in range(n_src)])

    def hop_group(value, by):
        pairs = [(i, i // group * group + (i + by) % group) for i in range(n_src)]
        return lax.ppermute(value, "src", pairs)

    def hop_focus(value):
        return lax.ppermute(value, "focus", [(0, 1), (1, 0)])

    def hop_tile(value, by):
        def place(t, s, f):
            return (t * n_src + s) * n_focus + f

        pairs = []
        for t in range(n_tile - 1):
            for s in range(n_src):
                u = (s + by) % n_src
                pairs.append((place(t, s, 0), place(t + 1, u, 1)))
                pairs.append((place(t + 1, s, 1), place(t, u, 0)))
        return lax.ppermute(value, ("tile", "src", "focus"), pairs)

    got = []
    if group > 1:
        sends = call(
            lambda *refs: send_kernel(sources, lambda d: group_corner(d + 1), *refs),
            Shape(group - 1, local_src, freqs, 2 * freqs),
            [SMEM, VMEM],
        )(weights, pupil)
        got = [hop_group(sends[d - 1], d) for d in range(1, group)]
    edge = call(edge_kernel, Shape(freqs, 2 * freqs), [VMEM, VMEM, VMEM])(
        mask, tables["row"], tables["edge"]
    )
    near = hop_tile(edge, 0)
    spec, own_pack = call(
        lambda *refs: own_kernel(sources, group_corner, *refs),
        [(freqs, 2 * freqs), (local_src, freqs, 2 * freqs)],
        [SMEM, VMEM, VMEM, VMEM, VMEM],
        flops=10**9,
    )(weights, pupil, mask, tables["row"], tables["colt"])
    specs = [spec, near, hop_focus(near)]

    gradient = []
    for c in range(n_corner):
        if group > 1:
            packs = [own_pack] + got
        else:
            packs = [
                call(
                    lambda *refs: send_kernel(sources, fixed_corner(c), *refs),
                    Shape(1, local_src, freqs, 2 * freqs),
                    [SMEM, VMEM],
                )(weights, pupil)[0]
            ]

        def corner_of(c=c):
            mine = group_corner(0) if group > 1 else c
            return lax.axis_index("focus") * corner_dev + mine

        n_pack = len(packs)
        field = (n_pack * local_src, grid, 2 * grid)
        if n_src == group:
            gs = call(
                lambda *refs: main_kernel(len(specs), n_pack, corner_of, *refs),
                Shape(freqs, 2 * freqs),
                [SMEM] + [VMEM] * (len(specs) + n_pack + 7),
                [pltpu.VMEM(field, jnp.float32)],
                limit=24,
            )(
                counts,
                *specs,
                *packs,
                target,
                *(tables[k] for k in ("right1", "right1t", "left2", "back2", "up", "upt")),
            )
        else:
            part, fields = call(
                lambda *refs: forward_kernel(len(specs), n_pack, *refs),
                [(grid, grid), field],
                [VMEM] * (len(specs) + n_pack + 2),
                limit=24,
            )(*specs, *packs, tables["right1"], tables["left2"])
            parts = [part] + [hop_src(part, r) for r in range(group, n_src, group)]
            gs = call(
                lambda *refs: adjoint_kernel(len(parts), n_pack, corner_of, *refs),
                Shape(freqs, 2 * freqs),
                [SMEM] + [VMEM] * (len(parts) + n_pack + 6),
                limit=24,
            )(
                counts,
                *parts,
                *packs,
                target,
                *(tables[k] for k in ("right1t", "back2", "up", "upt")),
                fields,
            )
        gradient.append(gs)
    gs = sum(gradient[1:]) + gradient[0] if len(gradient) > 1 else gradient[0]
    gs = gs + hop_focus(gs)
    gs = sum([hop_src(gs, d) for d in range(1, n_src)], gs)
    received = hop_tile(gs, 0)
    across = hop_focus(received)
    rows = tile // (n_src * n_focus)
    return call(
        lambda *refs: final_kernel(1, 1, *refs),
        Shape(rows, tile),
        [VMEM] * 6,
    )(gs, received, across, *(tables[k] for k in ("rowt", "colown", "coledge")))


def solution(mesh):
    return jax.shard_map(
        per_device,
        mesh=mesh,
        in_specs=(
            P("parts", "tile"),
            P("parts", "tile"),
            P(None, "src", "focus", None, None),
            P("src"),
            P("parts"),
        ),
        out_specs=P(("parts", "src", "focus"), "tile"),
        check_vma=False,
    )
```

```python
import math

import jax
import jax.numpy as jnp
import numpy as np
from jax import lax
from jax.experimental import pallas as pl
from jax.experimental.pallas import tpu as pltpu
from jax.sharding import PartitionSpec as P

AMBIT = 64

RESIST_SLOPE = 4.0
RESIST_LEVEL = 0.5

BATCH = 4

VMEM = pl.BlockSpec(memory_space=pltpu.VMEM)
SMEM = pl.BlockSpec(memory_space=pltpu.SMEM)


def halves(value):
    value = np.asarray(value, np.float32)
    high = value.astype(jnp.bfloat16)
    low = (value - high.astype(np.float32)).astype(jnp.bfloat16)
    return np.stack([high, low])


def split(value):
    high = value.astype(jnp.bfloat16)
    low = (value - high.astype(jnp.float32)).astype(jnp.bfloat16)
    return high, low


def mm(left, right):
    return lax.dot_general(
        left, right, (((1,), (0,)), ((), ())), preferred_element_type=jnp.float32
    )


def mm3(left, right):
    lh, ll = left
    rh, rl = right
    return mm(jnp.concatenate([lh, ll, lh], axis=1), jnp.concatenate([rh, rh, rl], axis=0))


def phase(freqs, length, positions):
    k = np.arange(freqs) - freqs // 2
    angle = np.mod(k[:, None] * np.asarray(positions)[None, :], length) * (2.0 * math.pi / length)
    return np.cos(angle), np.sin(angle)


def make_tables(tile, freqs, width):
    win = tile + 2 * width
    grid = 2 * freqs
    norm_win = 1.0 / math.sqrt(win)
    norm_back = math.sqrt(2.0 / freqs)
    cos_col, sin_col = phase(freqs, win, np.arange(win))
    col_re, col_im = cos_col * norm_win, -sin_col * norm_win
    cos_row, sin_row = phase(freqs, win, np.arange(tile) + width)
    row_re, row_im = cos_row * norm_win, -sin_row * norm_win
    cos_grid, sin_grid = phase(freqs, grid, np.arange(grid))
    a_re, a_im = cos_grid.T * norm_back, sin_grid.T * norm_back

    row = np.concatenate([row_re, row_im], axis=0)
    colt = np.concatenate([col_re.T, col_im.T], axis=1)
    side = max(128, width)
    edge = np.zeros((2, side, 2 * freqs))
    edge[0, side - width :] = colt[:width]
    edge[1, :width] = colt[win - width :]

    right1 = np.block([[a_re.T, a_im.T], [-a_im.T, a_re.T]])
    left2 = np.concatenate([a_re, a_im], axis=0)
    back2 = np.concatenate([a_re.T, a_im.T], axis=0)

    q = np.arange(-(freqs - 1), freqs)
    at = (np.arange(tile) + width)[:, None] / win - np.arange(grid)[None, :] / grid
    up = np.cos(2.0 * math.pi * at[:, :, None] * q).sum(-1) / grid

    l2h, l2l = halves(left2)
    b2h, b2l = halves(back2)
    return dict(
        row=halves(row),
        colt=halves(colt[width : width + tile]),
        edge=np.stack([halves(edge[0]), halves(edge[1])]),
        right1=halves(right1),
        left2=np.concatenate([l2h, l2h, l2l], axis=1),
        back2=np.block([[b2h, b2h], [b2l, b2l]]),
        up=halves(up),
        upt=halves(up.T),
        rowt=halves(row.T),
        colown=halves(np.concatenate([col_re, col_im], 0)[:, width : width + tile]),
        coledge=np.stack([halves(edge[0].T), halves(edge[1].T)]),
    )


def swapped_halves(x):
    return pltpu.roll(x, x.shape[-1] // 2, x.ndim - 1)


def left_lanes(shape):
    return lax.broadcasted_iota(jnp.int32, shape, len(shape) - 1) < shape[-1] // 2


def as_spectrum(z):
    half = z.shape[0] // 2
    turned = swapped_halves(z[half:])
    return z[:half] + jnp.where(left_lanes(turned.shape), -turned, turned)


def pack(pupil_ref, source, corner, scale):
    re = pupil_ref[0, source, corner] * scale
    im = pupil_ref[1, source, corner] * scale
    return jnp.concatenate([re, im], axis=1)


def source_scale(weights_ref, source, sources):
    w = jnp.full((1, 1), weights_ref[source], jnp.float32)
    return jnp.sqrt(w / sources)


def send_kernel(sources, corner_of, weights_ref, pupil_ref, out_ref):
    for d in range(out_ref.shape[0]):
        for s in range(out_ref.shape[1]):
            scale = source_scale(weights_ref, s, sources)
            out_ref[d, s] = pack(pupil_ref, s, corner_of(d), scale)


def edge_kernel(mask_ref, row_ref, edge_ref, out_ref):
    side = edge_ref.shape[2]
    focus = lax.axis_index("focus")
    start = pl.multiple_of((1 - focus) * (mask_ref.shape[1] - side), 128)
    slab = split(mask_ref[:, pl.ds(start, side)])
    y = mm3((row_ref[0], row_ref[1]), slab)
    out_ref[...] = as_spectrum(mm3(split(y), (edge_ref[focus, 0], edge_ref[focus, 1])))


def own_kernel(
    sources, corner_of, weights_ref, pupil_ref, mask_ref, row_ref, colt_ref, spec_ref, pack_ref
):
    y = mm3((row_ref[0], row_ref[1]), split(mask_ref[...]))
    spec_ref[...] = as_spectrum(mm3(split(y), (colt_ref[0], colt_ref[1])))
    for s in range(pack_ref.shape[0]):
        scale = source_scale(weights_ref, s, sources)
        pack_ref[s] = pack(pupil_ref, s, corner_of(0), scale)


def fold(z, sign):
    half = z.shape[0] // 2
    return z[:half] + swapped_halves(z[half:]) * sign


def lane_sign(freqs):
    return jnp.where(left_lanes((1, 2 * freqs)), -1.0, 1.0)


def forward(spec, pupil_of, pairs, right1, left2_ref, field_ref, data_ref, rows_ref):
    freqs, lanes = spec.shape
    grid = lanes
    turned = swapped_halves(spec)
    low = left_lanes(spec.shape)
    spec_a = jnp.where(low, spec, turned)
    spec_b = jnp.where(low, -turned, spec)
    sign = lane_sign(freqs)
    left2 = left2_ref[...]
    batch = math.gcd(BATCH, pairs)

    def left_product(group):
        for j in range(batch):
            pair = group * batch + j
            high, low = [], []
            for half in range(2):
                p = pupil_of(pair, half)
                gh, gl = split(p * spec_a + swapped_halves(p) * spec_b)
                high.append(gh)
                low.append(gl)
            gh, gl = jnp.concatenate(high, axis=1), jnp.concatenate(low, axis=1)
            f = mm(left2, jnp.concatenate([gh, gl, gh], axis=0))
            for half in range(2):
                hh, hl = split(fold(f[:, half * lanes : (half + 1) * lanes], sign))
                rows_ref[2 * pair + half, :, :lanes] = hh
                rows_ref[2 * pair + half, :, lanes : 2 * lanes] = hl

    def right_product(group, total):
        size = 2 * batch
        rows = rows_ref[pl.ds(group * size, size), :, : 2 * lanes]
        rows = rows.reshape(size * grid, 2 * lanes)
        right = jnp.concatenate([right1[0][...], right1[0][...], right1[1][...]], axis=0)
        e = mm(jnp.concatenate([rows, rows[:, :lanes]], axis=1), right)
        for s in range(size):
            part = e[s * grid : (s + 1) * grid]
            field_ref[group * size + s] = part
            part = part * part
            total = total + (part[:, :grid] + part[:, grid:])
        return total

    def step(group, total):
        left_product(group + 1)
        return right_product(group, total)

    groups = pairs // batch
    left_product(0)
    total = lax.fori_loop(0, groups - 1, step, jnp.zeros((grid, grid), jnp.float32))
    return right_product(groups - 1, total)


def adjoint(
    intensity, target, active, pupil_of, pairs, right1t, back2_ref, up, upt, field_ref, data_ref, rows_ref
):
    grid = intensity.shape[0]
    freqs, lanes = grid // 2, grid
    up = (up[0][...], up[1][...])
    upt = (upt[0][...], upt[1][...])
    image = mm3(up, split(mm3(split(intensity * RESIST_SLOPE), upt)))
    resist = jax.nn.sigmoid(image - RESIST_SLOPE * RESIST_LEVEL)
    slope = (resist - target) * (resist * (1.0 - resist))
    down = mm3(upt, split(mm3(split(slope), up))) * (4.0 * RESIST_SLOPE * active)
    down2 = jnp.concatenate([down, down], axis=1)
    back2 = back2_ref[...]
    sign = -lane_sign(freqs)
    batch = math.gcd(BATCH, pairs)
    size = 2 * batch

    def right_product(group):
        high, low = [], []
        for j in range(size):
            eh, el = split(down2 * field_ref[group * size + j])
            high.append(eh)
            low.append(el)
        rows = jnp.concatenate(
            [jnp.concatenate(high, axis=0), jnp.concatenate(low, axis=0)], axis=1
        )
        both = jnp.concatenate([right1t[0][...], right1t[1][...]], axis=1)
        t = mm(rows, jnp.concatenate([both, both], axis=0))
        t = t[:, :lanes] + t[:, lanes:]
        for j in range(batch):
            for half in range(2):
                k = 2 * j + half
                hh, hl = split(t[k * grid : (k + 1) * grid])
                at = half * lanes
                data_ref[group * batch + j, :grid, at : at + lanes] = hh
                data_ref[group * batch + j, grid:, at : at + lanes] = hl

    def left_product(group, carry):
        t1, t2 = carry
        for j in range(batch):
            pair = group * batch + j
            f = mm(back2, data_ref[pair])
            f = f[: 2 * freqs] + f[2 * freqs :]
            for half in range(2):
                q = fold(f[:, half * lanes : (half + 1) * lanes], sign)
                p = pupil_of(pair, half)
                t1 = t1 + p * q
                t2 = t2 + swapped_halves(p) * q
        return t1, t2

    def step(group, carry):
        right_product(group + 1)
        return left_product(group, carry)

    groups = pairs // batch
    zero = jnp.zeros((freqs, lanes), jnp.float32)
    right_product(0)
    carry = lax.fori_loop(0, groups - 1, step, (zero, zero))
    t1, t2 = left_product(groups - 1, carry)
    low = left_lanes(t1.shape)
    return jnp.where(low, t1 + swapped_halves(t1), t2 - swapped_halves(t2))


def active_here(corner_of, counts_ref):
    used = counts_ref[lax.axis_index("tile")]
    return (corner_of() < used).astype(jnp.float32)


def pick(packs):
    if len(packs) == 1:
        return lambda pair, half: packs[0][2 * pair + half]
    return lambda pair, half: packs[half][pair]


def main_kernel(n_spec, n_pack, corner_of, counts_ref, *refs):
    specs, refs = refs[:n_spec], refs[n_spec:]
    packs, refs = refs[:n_pack], refs[n_pack:]
    target_ref, right1_ref, left2_ref, right1t_ref, back2_ref, up_ref, upt_ref = refs[:7]
    out_ref, field_ref, data_ref, rows_ref = refs[7:]
    spec = sum(ref[...] for ref in specs[1:]) + specs[0][...]
    pupil_of = pick(packs)
    count = n_pack * packs[0].shape[0] // 2
    work = (field_ref, data_ref, rows_ref)
    intensity = forward(spec, pupil_of, count, pair_of(right1_ref), left2_ref, *work)
    out_ref[...] = adjoint(
        intensity,
        target_ref[...],
        active_here(corner_of, counts_ref),
        pupil_of,
        count,
        pair_of(right1t_ref),
        back2_ref,
        pair_of(up_ref),
        pair_of(upt_ref),
        *work,
    )


def pair_of(ref):
    return ref.at[0], ref.at[1]


def forward_kernel(n_spec, n_pack, *refs):
    specs, refs = refs[:n_spec], refs[n_spec:]
    packs, refs = refs[:n_pack], refs[n_pack:]
    right1_ref, left2_ref, intensity_ref, field_ref, data_ref, rows_ref = refs
    spec = sum(ref[...] for ref in specs[1:]) + specs[0][...]
    count = n_pack * packs[0].shape[0] // 2
    intensity_ref[...] = forward(
        spec, pick(packs), count, pair_of(right1_ref), left2_ref, field_ref, data_ref, rows_ref
    )


def adjoint_kernel(n_part, n_pack, corner_of, counts_ref, *refs):
    parts, refs = refs[:n_part], refs[n_part:]
    packs, refs = refs[:n_pack], refs[n_pack:]
    target_ref, right1t_ref, back2_ref, up_ref, upt_ref, field_ref = refs[:6]
    out_ref, data_ref, rows_ref = refs[6:]
    out_ref[...] = adjoint(
        sum(ref[...] for ref in parts[1:]) + parts[0][...],
        target_ref[...],
        active_here(corner_of, counts_ref),
        pick(packs),
        n_pack * packs[0].shape[0] // 2,
        pair_of(right1t_ref),
        back2_ref,
        pair_of(up_ref),
        pair_of(upt_ref),
        field_ref,
        data_ref,
        rows_ref,
    )


def final_kernel(n_own, n_near, *refs):
    own, refs = refs[:n_own], refs[n_own:]
    near, refs = refs[:n_near], refs[n_near:]
    across_ref, rowt_ref, colown_ref, coledge_ref, out_ref = refs
    rows, tile = out_ref.shape
    side = coledge_ref.shape[3]
    focus = lax.axis_index("focus")
    strip = lax.axis_index("src") * lax.axis_size("focus") + focus
    start = pl.multiple_of(strip * rows, rows)
    rowt = (rowt_ref[0, pl.ds(start, rows)], rowt_ref[1, pl.ds(start, rows)])

    def lines(gs):
        turned = swapped_halves(gs)
        stack = jnp.concatenate([gs, jnp.where(left_lanes(gs.shape), turned, -turned)], axis=0)
        return split(mm3(rowt, split(stack)))

    received = sum(ref[...] for ref in near[1:]) + near[0][...]
    across = across_ref[...]
    first = focus == 0
    from_right = jnp.where(first, received, across)
    from_left = jnp.where(first, across, received)
    main = mm3(lines(sum(ref[...] for ref in own[1:]) + own[0][...]), (colown_ref[0], colown_ref[1]))
    high = mm3(lines(from_right), (coledge_ref[0, 0], coledge_ref[0, 1]))
    low = mm3(lines(from_left), (coledge_ref[1, 0], coledge_ref[1, 1]))
    out_ref[...] = main
    out_ref[:, :side] = out_ref[:, :side] + low
    out_ref[:, tile - side :] = out_ref[:, tile - side :] + high


def call(kernel, shapes, specs, scratch=(), flops=0, limit=8):
    many = isinstance(shapes, (list, tuple))
    return pl.pallas_call(
        kernel,
        cost_estimate=pl.CostEstimate(flops=flops, bytes_accessed=1 << 20, transcendentals=0),
        compiler_params=pltpu.CompilerParams(vmem_limit_bytes=limit << 20),
        out_shape=[jax.ShapeDtypeStruct(s, jnp.float32) for s in shapes]
        if many
        else jax.ShapeDtypeStruct(shapes.shape, jnp.float32),
        in_specs=specs,
        out_specs=[VMEM] * len(shapes) if many else VMEM,
        scratch_shapes=list(scratch),
    )


class Shape:
    def __init__(self, *shape):
        self.shape = shape


def per_device(mask, target, pupil, weights, counts):
    tile = mask.shape[0]
    freqs = pupil.shape[-1]
    grid = 2 * freqs
    local_src = weights.shape[0]
    corner_dev = pupil.shape[2]
    n_tile, n_src, n_focus = (lax.axis_size(a) for a in ("tile", "src", "focus"))
    sources = local_src * n_src
    group = corner_dev if n_src % corner_dev == 0 else 1
    n_corner = corner_dev // group
    assert n_focus == 2

    def group_corner(d):
        return lax.rem(lax.axis_index("src") + d, group)

    def fixed_corner(c):
        return lambda d: c

    tables = {name: jnp.asarray(value) for name, value in make_tables(tile, freqs, AMBIT).items()}
    tables["right1t"] = jnp.asarray(
        np.swapaxes(np.asarray(make_tables(tile, freqs, AMBIT)["right1"]), 1, 2)
    )

    def hop_src(value, by):
        return lax.ppermute(value, "src", [(i, (i + by) % n_src) for i in range(n_src)])

    def hop_group(value, by):
        pairs = [(i, i // group * group + (i + by) % group) for i in range(n_src)]
        return lax.ppermute(value, "src", pairs)

    def hop_focus(value):
        return lax.ppermute(value, "focus", [(0, 1), (1, 0)])

    def hop_tile(value, by):
        def place(t, s, f):
            return (t * n_src + s) * n_focus + f

        pairs = []
        for t in range(n_tile - 1):
            for s in range(n_src):
                u = (s + by) % n_src
                pairs.append((place(t, s, 0), place(t + 1, u, 1)))
                pairs.append((place(t + 1, s, 1), place(t, u, 0)))
        return lax.ppermute(value, ("tile", "src", "focus"), pairs)

    got = []
    if group > 1:
        sends = call(
            lambda *refs: send_kernel(sources, lambda d: group_corner(d + 1), *refs),
            Shape(group - 1, local_src, freqs, 2 * freqs),
            [SMEM, VMEM],
        )(weights, pupil)
        got = [hop_group(sends[d - 1], d) for d in range(1, group)]
    edge = call(edge_kernel, Shape(freqs, 2 * freqs), [VMEM, VMEM, VMEM])(
        mask, tables["row"], tables["edge"]
    )
    near = hop_tile(edge, 0)
    spec, own_pack = call(
        lambda *refs: own_kernel(sources, group_corner, *refs),
        [(freqs, 2 * freqs), (local_src, freqs, 2 * freqs)],
        [SMEM, VMEM, VMEM, VMEM, VMEM],
        flops=10**9,
    )(weights, pupil, mask, tables["row"], tables["colt"])
    specs = [spec, near, hop_focus(near)]

    gradient = []
    for c in range(n_corner):
        if group > 1:
            packs = [own_pack] + got
        else:
            packs = [
                call(
                    lambda *refs: send_kernel(sources, fixed_corner(c), *refs),
                    Shape(1, local_src, freqs, 2 * freqs),
                    [SMEM, VMEM],
                )(weights, pupil)[0]
            ]

        def corner_of(c=c):
            mine = group_corner(0) if group > 1 else c
            return lax.axis_index("focus") * corner_dev + mine

        if len(packs) > 2:
            packs = [jnp.concatenate(packs)]
        n_pack = len(packs)
        count = n_pack * local_src
        field = (count, grid, 2 * grid)
        work = [
            pltpu.VMEM((count // 2, 2 * grid, 2 * grid), jnp.bfloat16),
            pltpu.VMEM((count, grid, 2 * grid), jnp.bfloat16),
        ]
        before, after = ("right1", "left2"), ("right1t", "back2", "up", "upt")
        if n_src == group:
            gs = call(
                lambda *refs: main_kernel(len(specs), n_pack, corner_of, *refs),
                Shape(freqs, 2 * freqs),
                [SMEM] + [VMEM] * (len(specs) + n_pack + 7),
                [pltpu.VMEM(field, jnp.float32)] + work,
                limit=24,
            )(counts, *specs, *packs, target, *(tables[k] for k in before + after))
        else:
            part, fields = call(
                lambda *refs: forward_kernel(len(specs), n_pack, *refs),
                [(grid, grid), field],
                [VMEM] * (len(specs) + n_pack + 2),
                work,
                limit=24,
            )(*specs, *packs, *(tables[k] for k in before))
            parts = [part] + [hop_src(part, r) for r in range(group, n_src, group)]
            gs = call(
                lambda *refs: adjoint_kernel(len(parts), n_pack, corner_of, *refs),
                Shape(freqs, 2 * freqs),
                [SMEM] + [VMEM] * (len(parts) + n_pack + 6),
                work,
                limit=24,
            )(counts, *parts, *packs, target, *(tables[k] for k in after), fields)
        gradient.append(gs)
    gs = sum(gradient[1:]) + gradient[0] if len(gradient) > 1 else gradient[0]
    gs = gs + hop_focus(gs)
    gs = sum([hop_src(gs, d) for d in range(1, n_src)], gs)
    received = hop_tile(gs, 0)
    across = hop_focus(received)
    rows = tile // (n_src * n_focus)
    return call(
        lambda *refs: final_kernel(1, 1, *refs),
        Shape(rows, tile),
        [VMEM] * 6,
    )(gs, received, across, *(tables[k] for k in ("rowt", "colown", "coledge")))


def solution(mesh):
    return jax.shard_map(
        per_device,
        mesh=mesh,
        in_specs=(
            P("parts", "tile"),
            P("parts", "tile"),
            P(None, "src", "focus", None, None),
            P("src"),
            P("parts"),
        ),
        out_specs=P(("parts", "src", "focus"), "tile"),
        check_vma=False,
    )
```

```python
import math

import jax
import jax.numpy as jnp
import numpy as np
from jax import lax
from jax.experimental import pallas as pl
from jax.experimental.pallas import tpu as pltpu
from jax.sharding import PartitionSpec as P

AMBIT = 64

RESIST_SLOPE = 4.0
RESIST_LEVEL = 0.5

BATCH = 4

VMEM = pl.BlockSpec(memory_space=pltpu.VMEM)
SMEM = pl.BlockSpec(memory_space=pltpu.SMEM)
HBM = pl.BlockSpec(memory_space=pltpu.HBM)


def halves(value):
    value = np.asarray(value, np.float32)
    high = value.astype(jnp.bfloat16)
    low = (value - high.astype(np.float32)).astype(jnp.bfloat16)
    return np.stack([high, low])


def split(value):
    high = value.astype(jnp.bfloat16)
    low = (value - high.astype(jnp.float32)).astype(jnp.bfloat16)
    return high, low


def mm(left, right):
    return lax.dot_general(
        left, right, (((1,), (0,)), ((), ())), preferred_element_type=jnp.float32
    )


def mm3(left, right):
    lh, ll = left
    rh, rl = right
    return mm(jnp.concatenate([lh, ll, lh], axis=1), jnp.concatenate([rh, rh, rl], axis=0))


def phase(freqs, length, positions):
    k = np.arange(freqs) - freqs // 2
    angle = np.mod(k[:, None] * np.asarray(positions)[None, :], length) * (2.0 * math.pi / length)
    return np.cos(angle), np.sin(angle)


def make_tables(tile, freqs, width):
    win = tile + 2 * width
    grid = 2 * freqs
    norm_win = 1.0 / math.sqrt(win)
    norm_back = math.sqrt(2.0 / freqs)
    cos_col, sin_col = phase(freqs, win, np.arange(win))
    col_re, col_im = cos_col * norm_win, -sin_col * norm_win
    cos_row, sin_row = phase(freqs, win, np.arange(tile) + width)
    row_re, row_im = cos_row * norm_win, -sin_row * norm_win
    cos_grid, sin_grid = phase(freqs, grid, np.arange(grid))
    a_re, a_im = cos_grid.T * norm_back, sin_grid.T * norm_back

    row = np.concatenate([row_re, row_im], axis=0)
    colt = np.concatenate([col_re.T, col_im.T], axis=1)
    side = max(128, width)
    edge = np.zeros((2, side, 2 * freqs))
    edge[0, side - width :] = colt[:width]
    edge[1, :width] = colt[win - width :]

    right1 = np.block([[a_re.T, a_im.T], [-a_im.T, a_re.T]])
    left2 = np.concatenate([a_re, a_im], axis=0)
    back2 = np.concatenate([a_re.T, a_im.T], axis=0)

    q = np.arange(-(freqs - 1), freqs)
    at = (np.arange(tile) + width)[:, None] / win - np.arange(grid)[None, :] / grid
    up = np.cos(2.0 * math.pi * at[:, :, None] * q).sum(-1) / grid

    l2h, l2l = halves(left2)
    b2h, b2l = halves(back2)
    return dict(
        row=halves(row),
        colt=halves(colt[width : width + tile]),
        edge=np.stack([halves(edge[0]), halves(edge[1])]),
        right1=halves(right1),
        left2=np.concatenate([l2h, l2h, l2l], axis=1),
        back2=np.block([[b2h, b2h], [b2l, b2l]]),
        up=halves(up),
        upt=halves(up.T),
        rowt=halves(row.T),
        colown=halves(np.concatenate([col_re, col_im], 0)[:, width : width + tile]),
        coledge=np.stack([halves(edge[0].T), halves(edge[1].T)]),
    )


def swapped_halves(x):
    return pltpu.roll(x, x.shape[-1] // 2, x.ndim - 1)


def left_lanes(shape):
    return lax.broadcasted_iota(jnp.int32, shape, len(shape) - 1) < shape[-1] // 2


def as_spectrum(z):
    half = z.shape[0] // 2
    turned = swapped_halves(z[half:])
    return z[:half] + jnp.where(left_lanes(turned.shape), -turned, turned)


def pack(pupil_ref, source, corner, scale):
    re = pupil_ref[0, source, corner] * scale
    im = pupil_ref[1, source, corner] * scale
    return jnp.concatenate([re, im], axis=1)


def source_scale(weights_ref, source, sources):
    w = jnp.full((1, 1), weights_ref[source], jnp.float32)
    return jnp.sqrt(w / sources)


def send_kernel(sources, corner_of, weights_ref, pupil_ref, out_ref):
    for d in range(out_ref.shape[0]):
        for s in range(out_ref.shape[1]):
            scale = source_scale(weights_ref, s, sources)
            out_ref[d, s] = pack(pupil_ref, s, corner_of(d), scale)


def first_kernel(
    sources,
    corner_of,
    weights_hbm,
    pupil_hbm,
    mask_hbm,
    row_hbm,
    edge_hbm,
    edge_ref,
    out_ref,
    weights_ref,
    pupil_ref,
    mask_ref,
    row_ref,
    table_ref,
    sems,
):
    side = edge_hbm.shape[2]
    focus = lax.axis_index("focus")
    start = pl.multiple_of((1 - focus) * (mask_hbm.shape[1] - side), 128)
    sends = out_ref.shape[0]
    copies = [
        pltpu.make_async_copy(pupil_hbm.at[:, :, corner_of(d)], pupil_ref.at[d], sems.at[4 + d])
        for d in range(sends)
    ]
    copies += [
        pltpu.make_async_copy(weights_hbm, weights_ref, sems.at[0]),
        pltpu.make_async_copy(mask_hbm.at[:, pl.ds(start, side)], mask_ref, sems.at[1]),
        pltpu.make_async_copy(row_hbm, row_ref, sems.at[2]),
        pltpu.make_async_copy(edge_hbm.at[focus], table_ref, sems.at[3]),
    ]
    for copy in copies:
        copy.start()
    for copy in copies:
        copy.wait()
    for d in range(sends):
        for s in range(out_ref.shape[1]):
            scale = source_scale(weights_ref, s, sources)
            re, im = (pupil_ref[d, c, s] * scale for c in range(2))
            out_ref[d, s] = jnp.concatenate([re, im], axis=1)
    y = mm3((row_ref[0], row_ref[1]), split(mask_ref[...]))
    edge_ref[...] = as_spectrum(mm3(split(y), (table_ref[0], table_ref[1])))


def own_kernel(
    sources, corner_of, weights_ref, pupil_ref, mask_ref, row_ref, colt_ref, spec_ref, pack_ref
):
    y = mm3((row_ref[0], row_ref[1]), split(mask_ref[...]))
    spec_ref[...] = as_spectrum(mm3(split(y), (colt_ref[0], colt_ref[1])))
    for s in range(pack_ref.shape[0]):
        scale = source_scale(weights_ref, s, sources)
        pack_ref[s] = pack(pupil_ref, s, corner_of(0), scale)


def fold(z, sign):
    half = z.shape[0] // 2
    return z[:half] + swapped_halves(z[half:]) * sign


def lane_sign(freqs):
    return jnp.where(left_lanes((1, 2 * freqs)), -1.0, 1.0)


def forward(spec, pupil_of, pairs, right1, left2_ref, field_ref, data_ref, rows_ref):
    freqs, lanes = spec.shape
    grid = lanes
    turned = swapped_halves(spec)
    low = left_lanes(spec.shape)
    spec_a = jnp.where(low, spec, turned)
    spec_b = jnp.where(low, -turned, spec)
    sign = lane_sign(freqs)
    left2 = left2_ref[...]
    batch = math.gcd(BATCH, pairs)

    def left_product(group):
        for j in range(batch):
            pair = group * batch + j
            high, low = [], []
            for half in range(2):
                p = pupil_of(pair, half)
                gh, gl = split(p * spec_a + swapped_halves(p) * spec_b)
                high.append(gh)
                low.append(gl)
            gh, gl = jnp.concatenate(high, axis=1), jnp.concatenate(low, axis=1)
            f = mm(left2, jnp.concatenate([gh, gl, gh], axis=0))
            for half in range(2):
                hh, hl = split(fold(f[:, half * lanes : (half + 1) * lanes], sign))
                rows_ref[2 * pair + half, :, :lanes] = hh
                rows_ref[2 * pair + half, :, lanes : 2 * lanes] = hl

    def right_product(group, total):
        size = 2 * batch
        rows = rows_ref[pl.ds(group * size, size), :, : 2 * lanes]
        rows = rows.reshape(size * grid, 2 * lanes)
        right = jnp.concatenate([right1[0][...], right1[0][...], right1[1][...]], axis=0)
        e = mm(jnp.concatenate([rows, rows[:, :lanes]], axis=1), right)
        for s in range(size):
            part = e[s * grid : (s + 1) * grid]
            field_ref[group * size + s] = part
            part = part * part
            total = total + (part[:, :grid] + part[:, grid:])
        return total

    def step(group, total):
        left_product(group + 1)
        return right_product(group, total)

    groups = pairs // batch
    left_product(0)
    total = lax.fori_loop(0, groups - 1, step, jnp.zeros((grid, grid), jnp.float32))
    return right_product(groups - 1, total)


def adjoint(
    intensity, target, active, pupil_of, pairs, right1t, back2_ref, up, upt, field_ref, data_ref, rows_ref
):
    grid = intensity.shape[0]
    freqs, lanes = grid // 2, grid
    up = (up[0][...], up[1][...])
    upt = (upt[0][...], upt[1][...])
    image = mm3(up, split(mm3(split(intensity * RESIST_SLOPE), upt)))
    resist = jax.nn.sigmoid(image - RESIST_SLOPE * RESIST_LEVEL)
    slope = (resist - target) * (resist * (1.0 - resist))
    down = mm3(upt, split(mm3(split(slope), up))) * (4.0 * RESIST_SLOPE * active)
    down2 = jnp.concatenate([down, down], axis=1)
    back2 = back2_ref[...]
    sign = -lane_sign(freqs)
    batch = math.gcd(BATCH, pairs)
    size = 2 * batch

    def right_product(group):
        high, low = [], []
        for j in range(size):
            eh, el = split(down2 * field_ref[group * size + j])
            high.append(eh)
            low.append(el)
        rows = jnp.concatenate(
            [jnp.concatenate(high, axis=0), jnp.concatenate(low, axis=0)], axis=1
        )
        both = jnp.concatenate([right1t[0][...], right1t[1][...]], axis=1)
        t = mm(rows, jnp.concatenate([both, both], axis=0))
        t = t[:, :lanes] + t[:, lanes:]
        for j in range(batch):
            for half in range(2):
                k = 2 * j + half
                hh, hl = split(t[k * grid : (k + 1) * grid])
                at = half * lanes
                data_ref[group * batch + j, :grid, at : at + lanes] = hh
                data_ref[group * batch + j, grid:, at : at + lanes] = hl

    def left_product(group, carry):
        t1, t2 = carry
        for j in range(batch):
            pair = group * batch + j
            f = mm(back2, data_ref[pair])
            f = f[: 2 * freqs] + f[2 * freqs :]
            for half in range(2):
                q = fold(f[:, half * lanes : (half + 1) * lanes], sign)
                p = pupil_of(pair, half)
                t1 = t1 + p * q
                t2 = t2 + swapped_halves(p) * q
        return t1, t2

    def step(group, carry):
        right_product(group + 1)
        return left_product(group, carry)

    groups = pairs // batch
    zero = jnp.zeros((freqs, lanes), jnp.float32)
    right_product(0)
    carry = lax.fori_loop(0, groups - 1, step, (zero, zero))
    t1, t2 = left_product(groups - 1, carry)
    low = left_lanes(t1.shape)
    return jnp.where(low, t1 + swapped_halves(t1), t2 - swapped_halves(t2))


def fetch(counts_hbm, counts_ref, sem):
    copy = pltpu.make_async_copy(counts_hbm, counts_ref, sem)
    copy.start()
    return copy


def active_here(corner_of, counts_ref):
    used = counts_ref[lax.axis_index("tile")]
    return (corner_of() < used).astype(jnp.float32)


def pick(packs):
    if len(packs) == 1:
        return lambda pair, half: packs[0][2 * pair + half]
    return lambda pair, half: packs[half][pair]


def main_kernel(n_spec, n_pack, corner_of, counts_hbm, *refs):
    specs, refs = refs[:n_spec], refs[n_spec:]
    packs, refs = refs[:n_pack], refs[n_pack:]
    target_ref, right1_ref, left2_ref, right1t_ref, back2_ref, up_ref, upt_ref = refs[:7]
    out_ref, field_ref, data_ref, rows_ref, counts_ref, sem = refs[7:]
    copy = fetch(counts_hbm, counts_ref, sem)
    spec = sum(ref[...] for ref in specs[1:]) + specs[0][...]
    pupil_of = pick(packs)
    count = n_pack * packs[0].shape[0] // 2
    work = (field_ref, data_ref, rows_ref)
    intensity = forward(spec, pupil_of, count, pair_of(right1_ref), left2_ref, *work)
    copy.wait()
    out_ref[...] = adjoint(
        intensity,
        target_ref[...],
        active_here(corner_of, counts_ref),
        pupil_of,
        count,
        pair_of(right1t_ref),
        back2_ref,
        pair_of(up_ref),
        pair_of(upt_ref),
        *work,
    )


def pair_of(ref):
    return ref.at[0], ref.at[1]


def forward_kernel(n_spec, n_pack, *refs):
    specs, refs = refs[:n_spec], refs[n_spec:]
    packs, refs = refs[:n_pack], refs[n_pack:]
    right1_ref, left2_ref, intensity_ref, field_ref, data_ref, rows_ref = refs
    spec = sum(ref[...] for ref in specs[1:]) + specs[0][...]
    count = n_pack * packs[0].shape[0] // 2
    intensity_ref[...] = forward(
        spec, pick(packs), count, pair_of(right1_ref), left2_ref, field_ref, data_ref, rows_ref
    )


def adjoint_kernel(n_part, n_pack, corner_of, counts_hbm, *refs):
    parts, refs = refs[:n_part], refs[n_part:]
    packs, refs = refs[:n_pack], refs[n_pack:]
    target_ref, right1t_ref, back2_ref, up_ref, upt_ref, field_ref = refs[:6]
    out_ref, data_ref, rows_ref, counts_ref, sem = refs[6:]
    fetch(counts_hbm, counts_ref, sem).wait()
    out_ref[...] = adjoint(
        sum(ref[...] for ref in parts[1:]) + parts[0][...],
        target_ref[...],
        active_here(corner_of, counts_ref),
        pick(packs),
        n_pack * packs[0].shape[0] // 2,
        pair_of(right1t_ref),
        back2_ref,
        pair_of(up_ref),
        pair_of(upt_ref),
        field_ref,
        data_ref,
        rows_ref,
    )


def lines(gs, rowt_ref, rows):
    strip = lax.axis_index("src") * lax.axis_size("focus") + lax.axis_index("focus")
    start = pl.multiple_of(strip * rows, rows)
    rowt = (rowt_ref[0, pl.ds(start, rows)], rowt_ref[1, pl.ds(start, rows)])
    turned = swapped_halves(gs)
    stack = jnp.concatenate([gs, jnp.where(left_lanes(gs.shape), turned, -turned)], axis=0)
    return split(mm3(rowt, split(stack)))


def middle_kernel(gs_ref, rowt_ref, colown_ref, out_ref):
    out_ref[...] = mm3(
        lines(gs_ref[...], rowt_ref, out_ref.shape[0]), (colown_ref[0], colown_ref[1])
    )


def border_kernel(which_of, base_ref, gs_ref, rowt_ref, coledge_ref, out_ref):
    rows, tile = out_ref.shape
    side = coledge_ref.shape[3]
    which = which_of()
    part = mm3(
        lines(gs_ref[...], rowt_ref, rows), (coledge_ref[which, 0], coledge_ref[which, 1])
    )
    out_ref[...] = base_ref[...]
    at = pl.ds(pl.multiple_of((1 - which) * (tile - side), 128), side)
    out_ref[:, at] = out_ref[:, at] + part


def call(kernel, shapes, specs, scratch=(), flops=0, limit=8):
    many = isinstance(shapes, (list, tuple))
    return pl.pallas_call(
        kernel,
        cost_estimate=pl.CostEstimate(flops=flops, bytes_accessed=1 << 20, transcendentals=0),
        compiler_params=pltpu.CompilerParams(vmem_limit_bytes=limit << 20),
        out_shape=[jax.ShapeDtypeStruct(s, jnp.float32) for s in shapes]
        if many
        else jax.ShapeDtypeStruct(shapes.shape, jnp.float32),
        in_specs=specs,
        out_specs=[VMEM] * len(shapes) if many else VMEM,
        scratch_shapes=list(scratch),
    )


def in_hbm(x):
    return pltpu.with_memory_space_constraint(x, pltpu.HBM)


class Shape:
    def __init__(self, *shape):
        self.shape = shape


def per_device(mask, target, pupil, weights, counts):
    tile = mask.shape[0]
    freqs = pupil.shape[-1]
    grid = 2 * freqs
    local_src = weights.shape[0]
    corner_dev = pupil.shape[2]
    n_tile, n_src, n_focus = (lax.axis_size(a) for a in ("tile", "src", "focus"))
    sources = local_src * n_src
    group = corner_dev if n_src % corner_dev == 0 else 1
    n_corner = corner_dev // group
    assert n_focus == 2

    def group_corner(d):
        return lax.rem(lax.axis_index("src") + d, group)

    def fixed_corner(c):
        return lambda d: c

    tables = {name: jnp.asarray(value) for name, value in make_tables(tile, freqs, AMBIT).items()}
    tables["right1t"] = jnp.asarray(
        np.swapaxes(np.asarray(make_tables(tile, freqs, AMBIT)["right1"]), 1, 2)
    )

    def hop_src(value, by):
        return lax.ppermute(value, "src", [(i, (i + by) % n_src) for i in range(n_src)])

    def hop_group(value, by):
        pairs = [(i, i // group * group + (i + by) % group) for i in range(n_src)]
        return lax.ppermute(value, "src", pairs)

    def hop_focus(value):
        return lax.ppermute(value, "focus", [(0, 1), (1, 0)])

    def hop_tile(value, by):
        def place(t, s, f):
            return (t * n_src + s) * n_focus + f

        pairs = []
        for t in range(n_tile - 1):
            for s in range(n_src):
                u = (s + by) % n_src
                pairs.append((place(t, s, 0), place(t + 1, u, 1)))
                pairs.append((place(t + 1, s, 1), place(t, u, 0)))
        return lax.ppermute(value, ("tile", "src", "focus"), pairs)

    sends = group - 1
    side = tables["edge"].shape[2]
    edge, sent = call(
        lambda *refs: first_kernel(sources, lambda d: group_corner(d + 1), *refs),
        [(freqs, 2 * freqs), (max(sends, 1), local_src, freqs, 2 * freqs)],
        [HBM] * 5,
        [
            pltpu.SMEM(weights.shape, jnp.float32),
            pltpu.VMEM((max(sends, 1), 2, local_src, freqs, freqs), jnp.float32),
            pltpu.VMEM((tile, side), jnp.float32),
            pltpu.VMEM(tables["row"].shape, jnp.bfloat16),
            pltpu.VMEM(tables["edge"].shape[1:], jnp.bfloat16),
            pltpu.SemaphoreType.DMA((4 + max(sends, 1),)),
        ],
    )(*(in_hbm(x) for x in (weights, pupil, mask, tables["row"], tables["edge"])))
    got = [hop_group(sent[d - 1], d) for d in range(1, group)]
    near = hop_tile(edge, 0)
    spec, own_pack = call(
        lambda *refs: own_kernel(sources, group_corner, *refs),
        [(freqs, 2 * freqs), (local_src, freqs, 2 * freqs)],
        [SMEM, VMEM, VMEM, VMEM, VMEM],
        flops=10**9,
    )(weights, pupil, mask, tables["row"], tables["colt"])
    near, spec, own_pack = lax.optimization_barrier((near, spec, own_pack))
    specs = [spec, near, hop_focus(near)]

    gradient = []
    for c in range(n_corner):
        if group > 1:
            packs = [own_pack] + got
        else:
            packs = [
                call(
                    lambda *refs: send_kernel(sources, fixed_corner(c), *refs),
                    Shape(1, local_src, freqs, 2 * freqs),
                    [SMEM, VMEM],
                )(weights, pupil)[0]
            ]

        def corner_of(c=c):
            mine = group_corner(0) if group > 1 else c
            return lax.axis_index("focus") * corner_dev + mine

        if len(packs) > 2:
            packs = [jnp.concatenate(packs)]
        n_pack = len(packs)
        count = n_pack * local_src
        field = (count, grid, 2 * grid)
        work = [
            pltpu.VMEM((count // 2, 2 * grid, 2 * grid), jnp.bfloat16),
            pltpu.VMEM((count, grid, 2 * grid), jnp.bfloat16),
        ]
        used = [pltpu.SMEM(counts.shape, jnp.int32), pltpu.SemaphoreType.DMA]
        before, after = ("right1", "left2"), ("right1t", "back2", "up", "upt")
        if n_src == group:
            gs = call(
                lambda *refs: main_kernel(len(specs), n_pack, corner_of, *refs),
                Shape(freqs, 2 * freqs),
                [HBM] + [VMEM] * (len(specs) + n_pack + 7),
                [pltpu.VMEM(field, jnp.float32)] + work + used,
                limit=24,
            )(in_hbm(counts), *specs, *packs, target, *(tables[k] for k in before + after))
        else:
            part, fields = call(
                lambda *refs: forward_kernel(len(specs), n_pack, *refs),
                [(grid, grid), field],
                [VMEM] * (len(specs) + n_pack + 2),
                work,
                limit=24,
            )(*specs, *packs, *(tables[k] for k in before))
            parts = [part] + [hop_src(part, r) for r in range(group, n_src, group)]
            gs = call(
                lambda *refs: adjoint_kernel(len(parts), n_pack, corner_of, *refs),
                Shape(freqs, 2 * freqs),
                [HBM] + [VMEM] * (len(parts) + n_pack + 6),
                work + used,
                limit=24,
            )(in_hbm(counts), *parts, *packs, target, *(tables[k] for k in after), fields)
        gradient.append(gs)
    gs = sum(gradient[1:]) + gradient[0] if len(gradient) > 1 else gradient[0]
    gs = gs + hop_focus(gs)
    gs = sum([hop_src(gs, d) for d in range(1, n_src)], gs)
    rows = tile // (n_src * n_focus)
    received = hop_tile(gs, 0)
    out = call(middle_kernel, Shape(rows, tile), [VMEM] * 3, flops=10**9)(
        gs, tables["rowt"], tables["colown"]
    )
    received, out = lax.optimization_barrier((received, out))
    across = hop_focus(received)
    out = call(
        lambda *refs: border_kernel(lambda: lax.axis_index("focus"), *refs),
        Shape(rows, tile),
        [VMEM] * 4,
        flops=10**9,
    )(out, received, tables["rowt"], tables["coledge"])
    across, out = lax.optimization_barrier((across, out))
    return call(
        lambda *refs: border_kernel(lambda: 1 - lax.axis_index("focus"), *refs),
        Shape(rows, tile),
        [VMEM] * 4,
    )(out, across, tables["rowt"], tables["coledge"])


def solution(mesh):
    return jax.shard_map(
        per_device,
        mesh=mesh,
        in_specs=(
            P("parts", "tile"),
            P("parts", "tile"),
            P(None, "src", "focus", None, None),
            P("src"),
            P("parts"),
        ),
        out_specs=P(("parts", "src", "focus"), "tile"),
        check_vma=False,
    )
```
